256 devices in a mesh: pairs: 16 (over z, core), cols: 16 (over y, x).
Axes of the slice: x: 4, y: 4, z: 8, core: 2. Of those that a mesh axis runs over, the one named last changes fastest.
Arguments:
- pair_list: int32 [96, 5], P('pairs'), may hold values from 0 to 15, as said below
- near_tile_block: bfloat16 [96, 2048, 2048], P('pairs', None, 'cols'), may hold values from -0.0546875 to 0.0546875
- history: float32 [4, 32, 32, 2048], P(None, 'pairs', None, 'cols'), may hold values from -6 to 6
- excitation: float32 [4, 32, 32, 2048], P(None, 'pairs', None, 'cols'), may hold values from -6 to 6
- diagonal: float32 [32, 2048], P('pairs', 'cols'), may hold values from 2 to 4
Outputs:
- densities: float32 [4, 32, 32, 2048], P(None, 'pairs', None, 'cols')
The draws below stay inside these ranges and needn't reach their ends.
Inputs may be any that keep to these rules, and one draw needn't show every extreme that they name: `pair_list`: rows s * 6 to s * 6 + 5 are the slots of index s of pairs. Column 0 and column 2 are below 2, column 1 below 16, column 3 below 4, column 4 is 0 or 1. The live slots of a device come first and number at least 3; among them no value of column 1 appears more than 3 times, and some value exactly 3 times. One device has all 6 slots live.
All inputs are finite; a program needn't handle non-finite values.
Results may differ from the reference program's by a relative error of at most 0.0018.
Values may be sent and summed in bfloat16 or wider, within the bound.
A program may use at most 64 MiB of HBM per device.

```python
import jax
import jax.numpy as jnp
from jax import lax

CLUSTER_PATCHES = 2048
EXC = 32
DEL = 4
SM = 3
STEPS = 4
INDEX_CLUSTERS = 2
SLOTS_PER_INDEX = 6
GROUPS = 16
NCL = 32
TOTAL_SLOTS = 96


def draw_pair_list(key, part):
    full_key, device_key = jax.random.split(jax.random.fold_in(key, 7))
    full_device = jax.random.randint(full_key, (), 0, GROUPS)

    def one_device(index):
        keys = jax.random.split(jax.random.fold_in(device_key, index), 6)
        lowest = max(SM, SLOTS_PER_INDEX // 4)
        count = jax.random.randint(keys[0], (), lowest, SLOTS_PER_INDEX + 1)
        count = jnp.where(index == full_device, SLOTS_PER_INDEX, count)
        spots = jax.random.permutation(keys[1], GROUPS * SM)
        chosen = jax.random.randint(keys[2], (), 0, GROUPS)
        order = jnp.argsort((spots // SM != chosen).astype(jnp.int32), stable=True)
        owners = (spots[order][:SLOTS_PER_INDEX] // SM).astype(jnp.int32)
        first_local = jax.random.randint(keys[3], (SLOTS_PER_INDEX,), 0, INDEX_CLUSTERS)
        second_local = jax.random.randint(keys[4], (SLOTS_PER_INDEX,), 0, INDEX_CLUSTERS)
        delays = jax.random.randint(keys[5], (SLOTS_PER_INDEX,), 0, DEL)
        live = (jnp.arange(SLOTS_PER_INDEX) < count).astype(jnp.int32)
        return jnp.stack([first_local, owners, second_local, delays, live], axis=1).astype(jnp.int32)
    stacked_tiles = jax.vmap(one_device)(jnp.arange(GROUPS))
    return stacked_tiles.reshape(TOTAL_SLOTS, 5)


def shard_levels(rng, dims, cuts, least, high):
    level = 1.0
    for dim, shards_of in cuts:
        steps = jax.random.uniform(jax.random.fold_in(jax.random.fold_in(rng, 6), dim), (shards_of,), jnp.float32, least / len(cuts), high / len(cuts))
        level = level * jnp.repeat(jnp.exp(steps), dims[dim] // shards_of).reshape((-1,) + (1,) * (len(dims) - 1 - dim))
    return level


def normal_values(key, extent, scale, most, cuts=(), held_as=jnp.bfloat16):
    entries = scale * jax.random.normal(key, extent, jnp.float32)
    if cuts:
        entries = entries * shard_levels(key, extent, cuts, -0.22, 0.18)
    return jnp.clip(entries, -most, most).astype(held_as)


def setup_inputs(seed: int = 0) -> dict:
    streams_of = jax.random.split(jax.random.key(seed), 6)
    pair_list = draw_pair_list(jax.random.fold_in(streams_of[5], 71), 0)
    near_tile_block = normal_values(streams_of[1], (TOTAL_SLOTS, CLUSTER_PATCHES, CLUSTER_PATCHES), (2 * SLOTS_PER_INDEX * CLUSTER_PATCHES // INDEX_CLUSTERS) ** -0.5, 0.0546875, ((0, 16), (2, 16)))
    history = normal_values(streams_of[2], (DEL, NCL, EXC, CLUSTER_PATCHES), 1.0, 6.0, ((1, 16), (3, 16)), jnp.float32)
    excitation = normal_values(streams_of[3], (STEPS, NCL, EXC, CLUSTER_PATCHES), 1.0, 6.0, ((1, 16), (3, 16)), jnp.float32)
    diagonal = jnp.clip(2.0 + 2.0 * jax.random.uniform(streams_of[4], (NCL, CLUSTER_PATCHES), jnp.float32) ** shard_levels(streams_of[4], (NCL, CLUSTER_PATCHES), ((0, 16), (1, 16)), -0.2, 0.2), 2.0, 4.0)
    return dict(pair_list=pair_list, near_tile_block=near_tile_block, history=history, excitation=excitation, diagonal=diagonal)


def reference(pair_list, near_tile_block, history, excitation, diagonal):
    owning_row_list = (jnp.arange(TOTAL_SLOTS) // SLOTS_PER_INDEX).astype(jnp.int32)
    first_cluster = (owning_row_list * INDEX_CLUSTERS + pair_list[:, 0]).astype(jnp.int32)
    second_cluster = (pair_list[:, 1] * INDEX_CLUSTERS + pair_list[:, 2]).astype(jnp.int32)
    delay_index = pair_list[:, 3].astype(jnp.int32)
    weights = pair_list[:, 4].astype(jnp.float32)
    results = []
    for step in range(STEPS):
        rounded = history.astype(jnp.bfloat16)

        def visit(field, item):
            tile, first, second, delay, weight = item
            tile_wide = tile.astype(jnp.float32)
            near_first = rounded[delay, first].astype(jnp.float32)
            near_second = rounded[delay, second].astype(jnp.float32)
            forward = jnp.dot(near_second, tile_wide.T, precision=lax.Precision.HIGHEST)
            backward = jnp.dot(near_first, tile_wide, precision=lax.Precision.HIGHEST)
            field = field.at[first].add(weight * forward)
            field = field.at[second].add(weight * backward)
            return field, None

        start = jnp.zeros((NCL, EXC, CLUSTER_PATCHES), jnp.float32)
        field, unused = lax.scan(visit, start, (near_tile_block, first_cluster, second_cluster, delay_index, weights))
        fresh = (excitation[step] - field) / diagonal[:, None, :]
        results.append(fresh)
        history = jnp.concatenate([fresh[None], history[:-1]], axis=0)
    return jnp.stack(results)
```

```python
import functools
import math

import jax
import jax.numpy as jnp
from jax import lax
from jax.experimental import pallas as pl
from jax.experimental.pallas import tpu as pltpu
from jax.sharding import PartitionSpec as P

MESH = pl.DeviceIdType.MESH
STEPS = 4
DEL = 4
WIRE = jnp.bfloat16


def ring_distance(offset, size):
    return min(offset, size - offset)


def kernel(
    sizes,
    pair_ref,
    tile_hbm,
    history_hbm,
    excitation_hbm,
    diagonal_hbm,
    out_ref,
    tiles,
    history,
    excitation,
    diagonal,
    by_owner,
    by_col,
    lhs,
    weight,
    product,
    own_back,
    forward_out,
    forward_in,
    sibling_out,
    sibling_in,
    back_out,
    back_in,
    local_sem,
    owner_recv,
    owner_send,
    share_recv,
    share_send,
    col_recv,
    col_send,
    forward_recv,
    forward_send,
    sibling_recv,
    sibling_send,
    back_recv,
    back_send,
):
    depth, rows_y, rows_x, slots, clusters = sizes
    cols = rows_y * rows_x
    width = 128
    pair = lax.axis_index("pairs")
    col = lax.axis_index("cols")
    z, core = pair // 2, lax.rem(pair, 2)
    y, x = col // rows_x, lax.rem(col, rows_x)
    sibling = (z * 2 + 1 - core, col)

    def at_z(dz):
        return lax.rem(z + dz, depth) * 2 + core

    def at_col(dy, dx):
        return lax.rem(y + dy, rows_y) * rows_x + lax.rem(x + dx, rows_x)

    z_far = sorted(range(1, depth), key=lambda d: -ring_distance(d, depth))
    z_near = z_far[::-1]
    col_far = sorted(
        [(dy, dx) for dy in range(rows_y) for dx in range(rows_x)],
        key=lambda d: -ring_distance(d[0], rows_y) - ring_distance(d[1], rows_x),
    )
    peers = [(at_z(dz), col) for dz in z_far] + [sibling]
    peers += [(pair, at_col(dy, dx)) for dy, dx in col_far if (dy, dx) != (0, 0)]

    barrier = pltpu.get_barrier_semaphore()
    for peer in peers:
        pl.semaphore_signal(barrier, inc=1, device_id=peer, device_id_type=MESH)

    loads = [pltpu.make_async_copy(history_hbm, history, local_sem.at[slots])]
    loads += [
        pltpu.make_async_copy(
            tile_hbm.at[s], tiles.at[:, pl.ds(s * width, width)], local_sem.at[s]
        )
        for s in range(slots)
    ]
    loads += [
        pltpu.make_async_copy(excitation_hbm, excitation, local_sem.at[slots + 1]),
        pltpu.make_async_copy(diagonal_hbm, diagonal, local_sem.at[slots + 2]),
    ]
    for load in loads:
        load.start()

    for s in range(slots):
        key = jnp.where(
            pair_ref[s, 4] == 1, pair_ref[s, 1] * clusters + pair_ref[s, 2], -1
        )
        for side in range(2):
            for dz in range(depth):
                owner = lax.rem(z + dz, depth) * 2 + (core if side == 0 else 1 - core)
                for l in range(clusters):
                    weight[((side * depth + dz) * clusters + l) * slots + s] = jnp.where(
                        key == owner * clusters + l, 1.0, 0.0
                    ).astype(jnp.float32)

    loads[0].wait()
    for d in range(DEL):
        rounded = history[d].astype(jnp.bfloat16)
        by_owner[DEL - 1 - d, pair] = rounded
        by_col[DEL - 1 - d, col] = rounded

    pl.semaphore_wait(barrier, len(peers))

    def copy(src, dst, send, recv, device):
        return pltpu.make_async_remote_copy(
            src_ref=src,
            dst_ref=dst,
            send_sem=send,
            recv_sem=recv,
            device_id=device,
            device_id_type=MESH,
        )

    def send_density(phase, first, count):
        times = pl.ds(first, count)
        source = by_owner.at[times, pair]
        for dz in z_far:
            copy(
                source,
                by_owner.at[times, pair],
                owner_send.at[phase],
                owner_recv.at[phase, dz - 1],
                (at_z(dz), col),
            ).start()
        for dy, dx in col_far:
            if (dy, dx) != (0, 0):
                copy(
                    source,
                    by_col.at[times, col],
                    col_send.at[phase],
                    col_recv.at[phase],
                    (pair, at_col(dy, dx)),
                ).start()
        copy(
            source,
            by_owner.at[times, pair],
            share_send.at[phase],
            share_recv.at[phase],
            sibling,
        ).start()

    def wait_recv(ref, sem, send):
        copy(ref, ref, send, sem, sibling).wait_recv()

    def wait_send(ref, sem, recv):
        copy(ref, ref, sem, recv, sibling).wait_send()

    def step(t, first, count):
        times = pl.ds(first, count)
        for dz in z_near:
            source = at_z(depth - dz)
            block = by_owner.at[times, source]
            wait_recv(block, owner_recv.at[t, dz - 1], owner_send.at[t])
            copy(block, block, share_send.at[t], share_recv.at[t], sibling).start()
        wait_recv(by_col.at[times, pl.ds(0, cols - 1)], col_recv.at[t], col_send.at[t])

        for s in range(slots):
            when = t + DEL - 1 - pair_ref[s, 3]
            mine = pair_ref[s, 0]
            near = jnp.concatenate([by_col[when, c, mine] for c in range(cols)], axis=1)
            product[s] = jnp.dot(
                near,
                tiles[:, s * width : (s + 1) * width],
                preferred_element_type=jnp.float32,
            )
        for dz in range(depth):
            for l in range(clusters):
                for side in range(2):
                    base = ((side * depth + dz) * clusters + l) * slots
                    total = weight[base] * product[0]
                    for s in range(1, slots):
                        total += weight[base + s] * product[s]
                    if side == 0:
                        own_back[dz, l] = total
                    else:
                        sibling_out[t, dz, l] = total.astype(WIRE)

        wait_recv(by_owner.at[times, pl.ds(0, depth)], share_recv.at[t], share_send.at[t])
        for s in range(slots):
            when = t + DEL - 1 - pair_ref[s, 3]
            block = by_owner[when, pair_ref[s, 1], pair_ref[s, 2]]
            for l in range(clusters):
                chosen = (pair_ref[s, 4] == 1) & (pair_ref[s, 0] == l)
                lhs[l * 32 : (l + 1) * 32, s * width : (s + 1) * width] = jnp.where(
                    chosen, block, jnp.zeros_like(block)
                )
        copy(
            sibling_out.at[t],
            sibling_in.at[t],
            sibling_send.at[t],
            sibling_recv.at[t],
            sibling,
        ).start()

        field = None
        left = lhs[...]
        for dy, dx in col_far:
            rows = pl.ds(pl.multiple_of(at_col(dy, dx) * width, width), width)
            part = lax.dot_general(
                left,
                tiles[rows, :],
                (((1,), (1,)), ((), ())),
                preferred_element_type=jnp.float32,
            ).reshape(clusters, 32, width)
            if (dy, dx) == (0, 0):
                field = part
            else:
                index = dy * rows_x + dx - 1
                forward_out[t, index] = part.astype(WIRE)
                copy(
                    forward_out.at[t, index],
                    forward_in.at[t, index],
                    forward_send.at[t],
                    forward_recv.at[t],
                    (pair, at_col(dy, dx)),
                ).start()

        wait_recv(sibling_in.at[t], sibling_recv.at[t], sibling_send.at[t])
        for dz in z_far + [0]:
            total = own_back[dz] + sibling_in[t, dz].astype(jnp.float32)
            if dz == 0:
                field = field + total
            else:
                back_out[t, dz - 1] = total.astype(WIRE)
                copy(
                    back_out.at[t, dz - 1],
                    back_in.at[t, dz - 1],
                    back_send.at[t],
                    back_recv.at[t],
                    (at_z(dz), col),
                ).start()

        wait_recv(forward_in.at[t], forward_recv.at[t], forward_send.at[t])
        for index in range(cols - 1):
            field = field + forward_in[t, index].astype(jnp.float32)
        wait_recv(back_in.at[t], back_recv.at[t], back_send.at[t])
        for index in range(depth - 1):
            field = field + back_in[t, index].astype(jnp.float32)
        fresh = (excitation[t] - field) / diagonal[...][:, None, :]
        out_ref[t] = fresh
        return fresh

    def publish(t, fresh):
        rounded = fresh.astype(jnp.bfloat16)
        by_owner[DEL + t, pair] = rounded
        by_col[DEL + t, col] = rounded
        send_density(t + 1, DEL + t, 1)

    send_density(0, 0, DEL)
    for load in loads[1:]:
        load.wait()
    publish(0, step(0, 0, DEL))

    def later(t, carry):
        publish(t, step(t, DEL - 1 + t, 1))
        return carry

    lax.fori_loop(1, STEPS - 1, later, 0)
    step(STEPS - 1, DEL + STEPS - 2, 1)

    for t in range(STEPS):
        times = pl.ds(0, DEL) if t == 0 else pl.ds(DEL - 1 + t, 1)
        wait_send(by_owner.at[times, pl.ds(0, depth - 1)], owner_send.at[t], owner_recv.at[t, 0])
        wait_send(by_owner.at[times, pl.ds(0, depth)], share_send.at[t], share_recv.at[t])
        wait_send(by_col.at[times, pl.ds(0, cols - 1)], col_send.at[t], col_recv.at[t])
        wait_send(forward_out.at[t], forward_send.at[t], forward_recv.at[t])
        wait_send(sibling_out.at[t], sibling_send.at[t], sibling_recv.at[t])
        wait_send(back_out.at[t], back_send.at[t], back_recv.at[t])


def march(groups, cols, pair_list, near_tile_block, history, excitation, diagonal):
    slots, patches, width = near_tile_block.shape
    clusters, excite = history.shape[1:3]
    depth = groups // 2
    rows_y = rows_x = math.isqrt(cols)
    block = (clusters, excite, width)
    dma = pltpu.SemaphoreType.DMA
    anywhere = pl.BlockSpec(memory_space=pl.ANY)
    return pl.pallas_call(
        functools.partial(kernel, (depth, rows_y, rows_x, slots, clusters)),
        out_shape=jax.ShapeDtypeStruct((STEPS,) + block, jnp.float32),
        in_specs=[pl.BlockSpec(memory_space=pltpu.SMEM)] + [anywhere] * 4,
        out_specs=pl.BlockSpec(memory_space=pltpu.VMEM),
        scratch_shapes=[
            pltpu.VMEM((patches, slots * width), jnp.bfloat16),
            pltpu.VMEM((DEL,) + block, jnp.float32),
            pltpu.VMEM((STEPS,) + block, jnp.float32),
            pltpu.VMEM((clusters, width), jnp.float32),
            pltpu.VMEM((DEL + STEPS - 1, groups) + block, jnp.bfloat16),
            pltpu.VMEM((DEL + STEPS - 1, cols) + block, jnp.bfloat16),
            pltpu.VMEM((clusters * excite, slots * width), jnp.bfloat16),
            pltpu.SMEM((groups * clusters * slots,), jnp.float32),
            pltpu.VMEM((slots, excite, width), jnp.float32),
            pltpu.VMEM((depth,) + block, jnp.float32),
            pltpu.VMEM((STEPS, cols - 1) + block, WIRE),
            pltpu.VMEM((STEPS, cols - 1) + block, WIRE),
            pltpu.VMEM((STEPS, depth) + block, WIRE),
            pltpu.VMEM((STEPS, depth) + block, WIRE),
            pltpu.VMEM((STEPS, depth - 1) + block, WIRE),
            pltpu.VMEM((STEPS, depth - 1) + block, WIRE),
            dma((slots + 3,)),
            dma((STEPS, depth - 1)),
            dma((STEPS,)),
            dma((STEPS,)),
            dma((STEPS,)),
            dma((STEPS,)),
            dma((STEPS,)),
            dma((STEPS,)),
            dma((STEPS,)),
            dma((STEPS,)),
            dma((STEPS,)),
            dma((STEPS,)),
            dma((STEPS,)),
        ],
        compiler_params=pltpu.CompilerParams(collective_id=0, has_side_effects=True),
    )(pair_list, near_tile_block, history, excitation, diagonal)


def solution(mesh):
    placed = (
        P("pairs", None),
        P("pairs", None, "cols"),
        P(None, "pairs", None, "cols"),
        P(None, "pairs", None, "cols"),
        P("pairs", "cols"),
    )
    return jax.shard_map(
        functools.partial(march, mesh.shape["pairs"], mesh.shape["cols"]),
        mesh=mesh,
        in_specs=placed,
        out_specs=P(None, "pairs", None, "cols"),
        check_vma=False,
    )
```

```python
import functools
import math

import jax
import jax.numpy as jnp
from jax import lax
from jax.experimental import pallas as pl
from jax.experimental.pallas import tpu as pltpu
from jax.sharding import PartitionSpec as P

MESH = pl.DeviceIdType.MESH
STEPS = 4
DEL = 4
SM = 3
AHEAD = 2
WIRE = jnp.bfloat16


def ring_distance(offset, size):
    return min(offset, size - offset)


def kernel(
    sizes,
    pair_ref,
    tile_hbm,
    history_hbm,
    excitation_hbm,
    diagonal_hbm,
    out_ref,
    tiles,
    turned,
    history,
    excitation,
    diagonal,
    by_owner,
    near_col,
    far_col,
    drain,
    lhs,
    table,
    product,
    own_back,
    forward_out,
    forward_in,
    sibling_out,
    sibling_in,
    back_out,
    back_in,
    local_sem,
    density_send,
    col_send,
    sum_send,
    early_owner,
    early_share,
    early_col,
    owner_recv,
    share_recv,
    col_recv,
    forward_recv,
    sibling_recv,
    back_recv,
):
    depth, rows_y, rows_x, slots, clusters = sizes
    cols = rows_y * rows_x
    width = 128
    pair = lax.axis_index("pairs")
    col = lax.axis_index("cols")
    z, core = pair // 2, lax.rem(pair, 2)
    y, x = col // rows_x, lax.rem(col, rows_x)
    sibling = (z * 2 + 1 - core, col)

    def at_z(dz):
        return lax.rem(z + dz, depth) * 2 + core

    def at_col(dy, dx):
        return lax.rem(y + dy, rows_y) * rows_x + lax.rem(x + dx, rows_x)

    def z_distance(dz):
        return ring_distance(dz, depth)

    def col_distance(d):
        return ring_distance(d[0], rows_y) + ring_distance(d[1], rows_x)

    z_near = sorted(range(1, depth), key=z_distance)
    z_far = z_near[::-1]
    col_near = sorted(
        [(dy, dx) for dy in range(rows_y) for dx in range(rows_x)][1:], key=col_distance
    )
    col_far = col_near[::-1]
    z_close = sum(z_distance(d) <= 2 for d in z_near)
    col_close = sum(col_distance(d) <= 2 for d in col_near)
    peers = [(at_z(dz), col) for dz in z_far] + [sibling]
    peers += [(pair, at_col(dy, dx)) for dy, dx in col_far]

    barrier = pltpu.get_barrier_semaphore()
    for peer in peers:
        pl.semaphore_signal(barrier, inc=1, device_id=peer, device_id_type=MESH)

    loads = [
        pltpu.make_async_copy(history_hbm, history, local_sem.at[0]),
        pltpu.make_async_copy(excitation_hbm, excitation, local_sem.at[1]),
        pltpu.make_async_copy(diagonal_hbm, diagonal, local_sem.at[2]),
    ]
    for load in loads:
        load.start()
    for s in range(slots):
        pltpu.make_async_copy(
            tile_hbm.at[s], tiles.at[:, pl.ds(s * width, width)], local_sem.at[3]
        ).start()

    loads[0].wait()
    for d in range(DEL):
        rounded = history[d].astype(jnp.bfloat16)
        by_owner[DEL - 1 - d, pair] = rounded
        near_col[DEL - 1 - d, 0] = rounded

    pl.semaphore_wait(barrier, len(peers))

    def copy(src, dst, send, recv, device):
        return pltpu.make_async_remote_copy(
            src_ref=src,
            dst_ref=dst,
            send_sem=send,
            recv_sem=recv,
            device_id=device,
            device_id_type=MESH,
        )

    def arrival(times, index):
        if index < col_close:
            return near_col.at[times, index + 1]
        return far_col.at[times, index - col_close]

    def send_density(times, owner_sem, share_sem, col_sem):
        source = by_owner.at[times, pair]
        for dz in z_far:
            copy(source, source, density_send, owner_sem(dz - 1), (at_z(dz), col)).start()
        for dy, dx in col_far:
            index = col_near.index((dy, dx))
            group = 0 if index < col_close else 1
            target = (pair, at_col(dy, dx))
            copy(source, arrival(times, index), col_send, col_sem(group), target).start()
        copy(source, source, density_send, share_sem, sibling).start()

    def wait_recv(ref, sem):
        copy(ref, ref, density_send, sem, sibling).wait_recv()

    def share(times, dz, owner_sem, share_sem):
        block = by_owner.at[times, at_z(depth - dz)]
        wait_recv(block, owner_sem(dz - 1))
        copy(block, block, density_send, share_sem, sibling).start()

    def send_step(t):
        send_density(
            pl.ds(DEL - 1 + t, 1),
            lambda k: owner_recv.at[t, k],
            share_recv.at[t],
            lambda k: col_recv.at[t, k],
        )

    def early_owner_sem(k):
        return early_owner.at[k]

    def early_col_sem(k):
        return early_col.at[k]

    past = pl.ds(0, DEL - 1)
    send_density(past, early_owner_sem, early_share, early_col_sem)
    send_step(0)

    keys = [
        jnp.where(pair_ref[s, 4] == 1, pair_ref[s, 1] * clusters + pair_ref[s, 2], -1)
        for s in range(slots)
    ]

    def place(n, carry):
        side, rest = n // (depth * clusters), lax.rem(n, depth * clusters)
        dz, l = rest // clusters, lax.rem(rest, clusters)
        owner = lax.rem(z + dz, depth) * 2 + lax.rem(core + side, 2)
        count = jnp.int32(0)
        found = [jnp.int32(slots)] * SM
        for s in range(slots):
            hit = keys[s] == owner * clusters + l
            found = [jnp.where(hit & (count == k), s, found[k]) for k in range(SM)]
            count = jnp.where(hit, count + 1, count)
        for k in range(SM):
            table[n * SM + k] = found[k]
        return carry

    lax.fori_loop(0, 2 * depth * clusters, place, 0)
    product[slots] = jnp.zeros_like(product[slots])
    for load in loads[1:]:
        load.wait()
    pltpu.make_async_copy(tiles, tiles, local_sem.at[3]).wait()

    def turn(c, carry):
        turned[c] = tiles[pl.ds(pl.multiple_of(c * width, width), width), :].T
        return carry

    lax.fori_loop(0, cols, turn, 0)

    for dz in z_near:
        share(past, dz, early_owner_sem, early_share)
    wait_recv(near_col.at[past, pl.ds(1, col_close)], early_col.at[0])
    if col_close < cols - 1:
        wait_recv(far_col.at[past], early_col.at[1])
    wait_recv(by_owner.at[past, pl.ds(0, depth)], early_share)

    def tile_rows(offset):
        source = at_col(rows_y - offset[0], rows_x - offset[1])
        return pl.ds(pl.multiple_of(source * width, width), width)

    def backward(s, t, blocks, offsets):
        when = t + DEL - 1 - pair_ref[s, 3]
        mine = pair_ref[s, 0]
        total = None
        for first in range(0, len(offsets), 2):
            span = range(first, min(first + 2, len(offsets)))
            near = [blocks[when, k, mine] for k in span]
            tile = [tiles[tile_rows(offsets[k]), s * width : (s + 1) * width] for k in span]
            part = jnp.dot(
                jnp.concatenate(near, axis=1),
                jnp.concatenate(tile, axis=0),
                preferred_element_type=jnp.float32,
            )
            total = part if total is None else total + part
        return total

    def combine(side, dz, l):
        base = ((side * depth + dz) * clusters + l) * SM
        total = product[table[base]]
        for k in range(1, SM):
            total += product[table[base + k]]
        return total

    def step(t, carry):
        times = pl.ds(DEL - 1 + t, 1)

        def owner_sem(k):
            return owner_recv.at[t, k]

        for dz in z_near:
            if z_distance(dz) <= 3:
                share(times, dz, owner_sem, share_recv.at[t])
        wait_recv(near_col.at[times, pl.ds(1, col_close)], col_recv.at[t, 0])
        near_offsets = [(0, 0)] + col_near[:col_close]
        for s in range(slots):
            product[s] = backward(s, t, near_col, near_offsets)
        for dz in z_near:
            if z_distance(dz) > 3:
                share(times, dz, owner_sem, share_recv.at[t])
        far_offsets = col_near[col_close:]
        if far_offsets:
            wait_recv(far_col.at[times], col_recv.at[t, 1])
            for s in range(slots):
                product[s] += backward(s, t, far_col, far_offsets)
        for dz in range(depth):
            for l in range(clusters):
                sibling_out[t, dz, l] = combine(1, dz, l).astype(WIRE)

        wait_recv(by_owner.at[times, pl.ds(0, depth)], share_recv.at[t])
        for s in range(slots):
            when = t + DEL - 1 - pair_ref[s, 3]
            block = by_owner[when, pair_ref[s, 1], pair_ref[s, 2]]
            for l in range(clusters):
                chosen = (pair_ref[s, 4] == 1) & (pair_ref[s, 0] == l)
                lhs[l * 32 : (l + 1) * 32, s * width : (s + 1) * width] = jnp.where(
                    chosen, block, jnp.zeros_like(block)
                )
        copy(
            sibling_out.at[t], sibling_in.at[t], sum_send, sibling_recv.at[t], sibling
        ).start()

        left = lhs[...]

        def forward(offset):
            return jnp.dot(
                left, turned[at_col(*offset)], preferred_element_type=jnp.float32
            ).reshape(clusters, 32, width)

        def send_forward(offset, part):
            index = col_near.index(offset)
            forward_out[t, index] = part.astype(WIRE)
            copy(
                forward_out.at[t, index],
                forward_in.at[t, index],
                sum_send,
                forward_recv.at[t, 0 if index < col_close else 1],
                (pair, at_col(*offset)),
            ).start()

        waiting = []
        for offset in col_far:
            waiting.append((offset, forward(offset)))
            if len(waiting) > AHEAD:
                send_forward(*waiting.pop(0))
        field = forward((0, 0))
        for item in waiting:
            send_forward(*item)
        for dz in range(depth):
            for l in range(clusters):
                own_back[dz, l] = combine(0, dz, l)

        wait_recv(sibling_in.at[t], sibling_recv.at[t])
        for dz in z_far:
            total = own_back[dz] + sibling_in[t, dz].astype(jnp.float32)
            index = z_near.index(dz)
            back_out[t, index] = total.astype(WIRE)
            copy(
                back_out.at[t, index],
                back_in.at[t, index],
                sum_send,
                back_recv.at[t, 0 if index < z_close else 1],
                (at_z(dz), col),
            ).start()
        field = field + own_back[0] + sibling_in[t, 0].astype(jnp.float32)

        def collect(field, ref, first, last, sem):
            if last > first:
                wait_recv(ref.at[t, pl.ds(first, last - first)], sem)
                for index in range(first, last):
                    field = field + ref[t, index].astype(jnp.float32)
            return field

        field = collect(field, forward_in, 0, col_close, forward_recv.at[t, 0])
        field = collect(field, back_in, 0, z_close, back_recv.at[t, 0])
        field = collect(field, forward_in, col_close, cols - 1, forward_recv.at[t, 1])
        field = collect(field, back_in, z_close, depth - 1, back_recv.at[t, 1])
        fresh = (excitation[t] - field) / diagonal[...][:, None, :]
        out_ref[t] = fresh

        @pl.when(t < STEPS - 1)
        def publish():
            rounded = fresh.astype(jnp.bfloat16)
            by_owner[DEL + t, pair] = rounded
            near_col[DEL + t, 0] = rounded
            send_step(t + 1)

        return carry

    lax.fori_loop(0, STEPS, step, 0)

    def sent(count, sem):
        copy(drain.at[pl.ds(0, count)], drain.at[pl.ds(0, count)], sem, early_share, sibling).wait_send()

    times = DEL + STEPS - 1
    sent(times * (2 * depth - 1), density_send)
    sent(times * (cols - 1), col_send)
    sent(STEPS * (cols - 1 + depth + depth - 1), sum_send)


def march(groups, cols, pair_list, near_tile_block, history, excitation, diagonal):
    slots, patches, width = near_tile_block.shape
    clusters, excite = history.shape[1:3]
    depth = groups // 2
    rows_y = rows_x = math.isqrt(cols)
    block = (clusters, excite, width)
    near = 1 + sum(
        0 < ring_distance(dy, rows_y) + ring_distance(dx, rows_x) <= 2
        for dy in range(rows_y)
        for dx in range(rows_x)
    )
    dma = pltpu.SemaphoreType.DMA
    anywhere = pl.BlockSpec(memory_space=pl.ANY)
    return pl.pallas_call(
        functools.partial(kernel, (depth, rows_y, rows_x, slots, clusters)),
        out_shape=jax.ShapeDtypeStruct((STEPS,) + block, jnp.float32),
        in_specs=[pl.BlockSpec(memory_space=pltpu.SMEM)] + [anywhere] * 4,
        out_specs=pl.BlockSpec(memory_space=pltpu.VMEM),
        scratch_shapes=[
            pltpu.VMEM((patches, slots * width), jnp.bfloat16),
            pltpu.VMEM((cols, slots * width, width), jnp.bfloat16),
            pltpu.VMEM((DEL,) + block, jnp.float32),
            pltpu.VMEM((STEPS,) + block, jnp.float32),
            pltpu.VMEM((clusters, width), jnp.float32),
            pltpu.VMEM((DEL + STEPS - 1, groups) + block, jnp.bfloat16),
            pltpu.VMEM((DEL + STEPS - 1, near) + block, jnp.bfloat16),
            pltpu.VMEM((DEL + STEPS - 1, max(cols - near, 1)) + block, jnp.bfloat16),
            pltpu.VMEM((STEPS * (cols + 2 * depth),) + block, WIRE),
            pltpu.VMEM((clusters * excite, slots * width), jnp.bfloat16),
            pltpu.SMEM((groups * clusters * SM,), jnp.int32),
            pltpu.VMEM((slots + 1, excite, width), jnp.float32),
            pltpu.VMEM((depth,) + block, jnp.float32),
            pltpu.VMEM((STEPS, cols - 1) + block, WIRE),
            pltpu.VMEM((STEPS, cols - 1) + block, WIRE),
            pltpu.VMEM((STEPS, depth) + block, WIRE),
            pltpu.VMEM((STEPS, depth) + block, WIRE),
            pltpu.VMEM((STEPS, depth - 1) + block, WIRE),
            pltpu.VMEM((STEPS, depth - 1) + block, WIRE),
            dma((4,)),
            dma,
            dma,
            dma,
            dma((depth - 1,)),
            dma,
            dma((2,)),
            dma((STEPS, depth - 1)),
            dma((STEPS,)),
            dma((STEPS, 2)),
            dma((STEPS, 2)),
            dma((STEPS,)),
            dma((STEPS, 2)),
        ],
        compiler_params=pltpu.CompilerParams(collective_id=0, has_side_effects=True),
    )(pair_list, near_tile_block, history, excitation, diagonal)


def solution(mesh):
    placed = (
        P("pairs", None),
        P("pairs", None, "cols"),
        P(None, "pairs", None, "cols"),
        P(None, "pairs", None, "cols"),
        P("pairs", "cols"),
    )
    return jax.shard_map(
        functools.partial(march, mesh.shape["pairs"], mesh.shape["cols"]),
        mesh=mesh,
        in_specs=placed,
        out_specs=P(None, "pairs", None, "cols"),
        check_vma=False,
    )
```

```python
import functools
import math

import jax
import jax.numpy as jnp
from jax import lax
from jax.experimental import pallas as pl
from jax.experimental.pallas import tpu as pltpu
from jax.sharding import PartitionSpec as P

MESH = pl.DeviceIdType.MESH
STEPS = 4
DEL = 4
SM = 3
AHEAD = 2
WIRE = jnp.bfloat16


def ring_distance(offset, size):
    return min(offset, size - offset)


def kernel(
    sizes,
    pair_hbm,
    tile_hbm,
    history_hbm,
    excitation_hbm,
    diagonal_hbm,
    out_ref,
    pairs,
    tiles,
    turned,
    history,
    excitation,
    diagonal,
    by_z,
    near_col,
    far_col,
    drain,
    lhs,
    table,
    product,
    fresh_out,
    fresh_in,
    forward_out,
    forward_in,
    back_out,
    back_in,
    local_sem,
    swap_recv,
    swap_send,
    density_send,
    sum_send,
    fresh_send,
    fresh_recv,
    early_z,
    early_col,
    z_recv,
    col_recv,
    forward_recv,
    back_recv,
):
    depth, rows_y, rows_x, slots, clusters, half = sizes
    cols = rows_y * rows_x
    width = 128
    count = 2 * clusters
    stack = 2 * slots
    pair = lax.axis_index("pairs")
    col = lax.axis_index("cols")
    z, core = pair // 2, lax.rem(pair, 2)
    y, x = col // rows_x, lax.rem(col, rows_x)
    sibling = (z * 2 + 1 - core, col)

    def at_z(dz):
        return lax.rem(z + dz, depth)

    def z_device(dz):
        return (at_z(dz) * 2 + core, col)

    def at_col(dy, dx):
        return lax.rem(y + dy, rows_y) * rows_x + lax.rem(x + dx, rows_x)

    def z_distance(dz):
        return ring_distance(dz, depth)

    def col_distance(d):
        return ring_distance(d[0], rows_y) + ring_distance(d[1], rows_x)

    z_near = sorted(range(1, depth), key=z_distance)
    z_far = z_near[::-1]
    col_near = sorted(
        [(dy, dx) for dy in range(rows_y) for dx in range(rows_x)][1:], key=col_distance
    )
    col_far = col_near[::-1]
    z_close = sum(z_distance(d) <= 2 for d in z_near)
    col_close = sum(col_distance(d) <= 2 for d in col_near)
    peers = [z_device(dz) for dz in z_far] + [sibling]
    peers += [(pair, at_col(dy, dx)) for dy, dx in col_far]

    barrier = pltpu.get_barrier_semaphore()
    for peer in peers:
        pl.semaphore_signal(barrier, inc=1, device_id=peer, device_id_type=MESH)

    mine = pl.ds(core * clusters, clusters)
    kept = pl.ds(pl.multiple_of(core * half, half), half)
    given = pl.ds(pl.multiple_of((1 - core) * half, half), half)

    def column(s):
        return pl.ds(pl.multiple_of((core * slots + s) * width, width), width)

    loads = [
        pltpu.make_async_copy(
            history_hbm.at[:, :, kept, :], history.at[:, mine], local_sem.at[0]
        ),
        pltpu.make_async_copy(pair_hbm, pairs.at[core], local_sem.at[1]),
        pltpu.make_async_copy(
            excitation_hbm.at[:, :, kept, :], excitation.at[:, mine], local_sem.at[2]
        ),
        pltpu.make_async_copy(diagonal_hbm, diagonal.at[core], local_sem.at[3]),
    ]
    for load in loads:
        load.start()
    for s in range(slots):
        pltpu.make_async_copy(
            tile_hbm.at[s], tiles.at[:, column(s)], local_sem.at[4]
        ).start()

    def round_history(who):
        part = pl.ds(who * clusters, clusters)
        for d in range(DEL):
            rounded = history[d, part].astype(jnp.bfloat16)
            by_z[DEL - 1 - d, z, part] = rounded
            near_col[DEL - 1 - d, 0, part] = rounded

    loads[0].wait()
    round_history(core)

    pl.semaphore_wait(barrier, len(peers))

    def copy(src, dst, send, recv, device):
        return pltpu.make_async_remote_copy(
            src_ref=src,
            dst_ref=dst,
            send_sem=send,
            recv_sem=recv,
            device_id=device,
            device_id_type=MESH,
        )

    swaps = [
        copy(
            history_hbm.at[:, :, given, :],
            history.at[:, mine],
            swap_send.at[0],
            swap_recv.at[0],
            sibling,
        ),
        copy(pair_hbm, pairs.at[core], swap_send.at[1], swap_recv.at[1], sibling),
        copy(
            excitation_hbm.at[:, :, given, :],
            excitation.at[:, mine],
            swap_send.at[2],
            swap_recv.at[2],
            sibling,
        ),
        copy(diagonal_hbm, diagonal.at[core], swap_send.at[3], swap_recv.at[3], sibling),
    ]
    for swap in swaps:
        swap.start()

    def arrival(times, index, part):
        if index < col_close:
            return near_col.at[times, index + 1, part]
        return far_col.at[times, index - col_close, part]

    def send_density(times, part, z_sem, col_sem):
        source = by_z.at[times, z, part]
        for dz in z_far:
            copy(source, source, density_send, z_sem, z_device(dz)).start()
        for offset in col_far:
            index = col_near.index(offset)
            group = 0 if index < col_close else 1
            target = (pair, at_col(*offset))
            sem = col_sem(group)
            copy(source, arrival(times, index, part), density_send, sem, target).start()

    def wait_recv(ref, sem):
        copy(ref, ref, density_send, sem, sibling).wait_recv()

    def early_col_sem(group):
        return early_col.at[group]

    past = pl.ds(0, DEL)
    send_density(past, mine, early_z, early_col_sem)
    for s in range(slots):
        copy(
            tile_hbm.at[s], tiles.at[:, column(s)], swap_send.at[4], swap_recv.at[4], sibling
        ).start()
    swaps[0].wait_recv()
    round_history(1 - core)
    send_density(past, pl.ds((1 - core) * clusters, clusters), early_z, early_col_sem)

    for load in loads[1:]:
        load.wait()
    for swap in swaps[1:]:
        swap.wait_recv()

    def field_of(s, k):
        return pairs[s // slots, s % slots, k]

    keys = [
        jnp.where(field_of(s, 4) == 1, field_of(s, 1) * clusters + field_of(s, 2), -1)
        for s in range(stack)
    ]

    def place(n, carry):
        dz, rest = n // count, lax.rem(n, count)
        key = at_z(dz) * count + rest
        seen = jnp.int32(0)
        found = [jnp.int32(stack)] * (2 * SM)
        for s in range(stack):
            hit = keys[s] == key
            found = [jnp.where(hit & (seen == k), s, found[k]) for k in range(2 * SM)]
            seen = jnp.where(hit, seen + 1, seen)
        for k in range(2 * SM):
            table[n * 2 * SM + k] = found[k]
        return carry

    lax.fori_loop(0, depth * count, place, 0)
    product[stack] = jnp.zeros_like(product[stack])

    def turn(who):
        part = pl.ds(pl.multiple_of(who * slots * width, width), slots * width)

        def body(c, carry):
            rows = pl.ds(pl.multiple_of(c * width, width), width)
            turned[c, part, :] = tiles[rows, part].T
            return carry

        lax.fori_loop(0, cols, body, 0)

    held = tiles.at[:, pl.ds(0, slots * width)]
    pltpu.make_async_copy(held, held, local_sem.at[4]).wait()
    turn(core)
    wait_recv(held, swap_recv.at[4])
    turn(1 - core)

    wait_recv(near_col.at[past, pl.ds(1, col_close)], early_col.at[0])
    if col_close < cols - 1:
        wait_recv(far_col.at[past], early_col.at[1])
    wait_recv(by_z.at[past, pl.ds(0, depth - 1)], early_z)

    def tile_rows(offset):
        source = at_col(rows_y - offset[0], rows_x - offset[1])
        return pl.ds(pl.multiple_of(source * width, width), width)

    def backward(s, t, blocks, offsets):
        when = t + DEL - 1 - field_of(s, 3)
        which = s // slots * clusters + field_of(s, 0)
        total = None
        for first in range(0, len(offsets), 2):
            span = range(first, min(first + 2, len(offsets)))
            near = [blocks[when, k, which] for k in span]
            tile = [tiles[tile_rows(offsets[k]), s * width : (s + 1) * width] for k in span]
            part = jnp.dot(
                jnp.concatenate(near, axis=1),
                jnp.concatenate(tile, axis=0),
                preferred_element_type=jnp.float32,
            )
            total = part if total is None else total + part
        return total

    def combine(dz, j):
        base = (dz * count + j) * 2 * SM
        total = product[table[base]]
        for k in range(1, 2 * SM):
            total += product[table[base + k]]
        return total

    def step(t, carry):
        times = pl.ds(DEL - 1 + t, 1)

        @pl.when(t > 0)
        def near_arrived():
            wait_recv(near_col.at[times, pl.ds(1, col_close)], col_recv.at[t, 0])

        near_offsets = [(0, 0)] + col_near[:col_close]
        for s in range(stack):
            product[s] = backward(s, t, near_col, near_offsets)

        @pl.when(t > 0)
        def z_arrived():
            wait_recv(by_z.at[times, pl.ds(0, depth - 1)], z_recv.at[t])

        for s in range(stack):
            when = t + DEL - 1 - field_of(s, 3)
            owner = field_of(s, 1)
            which = lax.rem(owner, 2) * clusters + field_of(s, 2)
            block = by_z[when, owner // 2, which]
            for l in range(clusters):
                chosen = (field_of(s, 4) == 1) & (field_of(s, 0) == l)
                for who in range(2):
                    row = (who * clusters + l) * half
                    value = jnp.zeros_like(block)
                    if who == s // slots:
                        value = jnp.where(chosen, block, value)
                    lhs[row : row + half, s * width : (s + 1) * width] = value

        far_offsets = col_near[col_close:]
        if far_offsets:

            @pl.when(t > 0)
            def far_arrived():
                wait_recv(far_col.at[times], col_recv.at[t, 1])

            for s in range(stack):
                product[s] += backward(s, t, far_col, far_offsets)

        for dz in z_far:
            index = z_near.index(dz)
            for j in range(count):
                back_out[t, index, j] = combine(dz, j).astype(WIRE)
            copy(
                back_out.at[t, index],
                back_in.at[t, index],
                sum_send,
                back_recv.at[t, 0 if index < z_close else 1],
                z_device(dz),
            ).start()

        left = lhs[...]

        def forward(offset):
            return jnp.dot(
                left, turned[at_col(*offset)], preferred_element_type=jnp.float32
            ).reshape(count, half, width)

        def send_forward(offset, part):
            index = col_near.index(offset)
            forward_out[t, index] = part.astype(WIRE)
            copy(
                forward_out.at[t, index],
                forward_in.at[t, index],
                sum_send,
                forward_recv.at[t, 0 if index < col_close else 1],
                (pair, at_col(*offset)),
            ).start()

        waiting = []
        for offset in col_far:
            waiting.append((offset, forward(offset)))
            if len(waiting) > AHEAD:
                send_forward(*waiting.pop(0))
        field = forward((0, 0))
        for item in waiting:
            send_forward(*item)
        field = field + jnp.stack([combine(0, j) for j in range(count)])

        def collect(field, ref, first, last, sem):
            if last > first:
                wait_recv(ref.at[t, pl.ds(first, last - first)], sem)
                for index in range(first, last):
                    field = field + ref[t, index].astype(jnp.float32)
            return field

        field = collect(field, back_in, 0, z_close, back_recv.at[t, 0])
        field = collect(field, back_in, z_close, depth - 1, back_recv.at[t, 1])
        field = collect(field, forward_in, 0, col_close, forward_recv.at[t, 0])
        field = collect(field, forward_in, col_close, cols - 1, forward_recv.at[t, 1])
        weights = diagonal[...].reshape(count, 1, width)
        fresh = (excitation[t] - field) / weights
        fresh_out[t] = fresh

        @pl.when(t < STEPS - 1)
        def publish():
            rounded = fresh.astype(jnp.bfloat16)
            by_z[DEL + t, z] = rounded
            near_col[DEL + t, 0] = rounded
            send_density(
                pl.ds(DEL + t, 1),
                pl.ds(0, count),
                z_recv.at[t + 1],
                lambda group: col_recv.at[t + 1, group],
            )

        copy(
            fresh_out.at[t, pl.ds((1 - core) * clusters, clusters)],
            fresh_in.at[t],
            fresh_send,
            fresh_recv,
            sibling,
        ).start()
        out_ref[t, :, kept, :] = fresh_out[t, mine]
        return carry

    lax.fori_loop(0, STEPS, step, 0)

    def sent(ref, sem):
        copy(ref, ref, sem, fresh_recv, sibling).wait_send()

    for swap in swaps:
        swap.wait_send()
    sent(held, swap_send.at[4])
    sent(drain.at[pl.ds(0, (DEL + STEPS - 1) * (depth - 1 + cols - 1))], density_send)
    sent(drain.at[pl.ds(0, STEPS * (depth - 1 + cols - 1))], sum_send)
    sent(fresh_in, fresh_send)
    wait_recv(fresh_in, fresh_recv)
    for t in range(STEPS):
        out_ref[t, :, given, :] = fresh_in[t]


def march(groups, cols, pair_list, near_tile_block, history, excitation, diagonal):
    slots, patches, width = near_tile_block.shape
    clusters, excite = history.shape[1:3]
    depth = groups // 2
    half = excite // 2
    rows_y = rows_x = math.isqrt(cols)
    near = 1 + sum(
        0 < ring_distance(dy, rows_y) + ring_distance(dx, rows_x) <= 2
        for dy in range(rows_y)
        for dx in range(rows_x)
    )
    block = (2 * clusters, half, width)
    dma = pltpu.SemaphoreType.DMA
    times = DEL + STEPS - 1
    anywhere = pl.BlockSpec(memory_space=pl.ANY)
    return pl.pallas_call(
        functools.partial(kernel, (depth, rows_y, rows_x, slots, clusters, half)),
        out_shape=OUT((STEPS, clusters, excite, width), jnp.float32),
        in_specs=[anywhere] * 5,
        out_specs=pl.BlockSpec(memory_space=pltpu.VMEM),
        scratch_shapes=[
            pltpu.SMEM((2,) + pair_list.shape, jnp.int32),
            pltpu.VMEM((patches, 2 * slots * width), jnp.bfloat16),
            pltpu.VMEM((cols, 2 * slots * width, width), jnp.bfloat16),
            pltpu.VMEM((DEL,) + block, jnp.float32),
            pltpu.VMEM((STEPS,) + block, jnp.float32),
            pltpu.VMEM((2, clusters, width), jnp.float32),
            pltpu.VMEM((times, depth) + block, jnp.bfloat16),
            pltpu.VMEM((times, near) + block, jnp.bfloat16),
            pltpu.VMEM((times, max(cols - near, 1)) + block, jnp.bfloat16),
            pltpu.VMEM((times * (depth + cols),) + block, WIRE),
            pltpu.VMEM((2 * clusters * half, 2 * slots * width), jnp.bfloat16),
            pltpu.SMEM((depth * 2 * clusters * 2 * SM,), jnp.int32),
            pltpu.VMEM((2 * slots + 1, half, width), jnp.float32),
            pltpu.VMEM((STEPS,) + block, jnp.float32),
            pltpu.VMEM((STEPS, clusters, half, width), jnp.float32),
            pltpu.VMEM((STEPS, cols - 1) + block, WIRE),
            pltpu.VMEM((STEPS, cols - 1) + block, WIRE),
            pltpu.VMEM((STEPS, depth - 1) + block, WIRE),
            pltpu.VMEM((STEPS, depth - 1) + block, WIRE),
            dma((5,)),
            dma((5,)),
            dma((5,)),
            dma,
            dma,
            dma,
            dma,
            dma,
            dma((2,)),
            dma((STEPS,)),
            dma((STEPS, 2)),
            dma((STEPS, 2)),
            dma((STEPS, 2)),
        ],
        compiler_params=pltpu.CompilerParams(collective_id=0, has_side_effects=True),
    )(pair_list, near_tile_block, history, excitation, diagonal)


OUT = pltpu.VMEM


def solution(mesh):
    placed = (
        P("pairs", None),
        P("pairs", None, "cols"),
        P(None, "pairs", None, "cols"),
        P(None, "pairs", None, "cols"),
        P("pairs", "cols"),
    )
    return jax.shard_map(
        functools.partial(march, mesh.shape["pairs"], mesh.shape["cols"]),
        mesh=mesh,
        in_specs=placed,
        out_specs=P(None, "pairs", None, "cols"),
        check_vma=False,
    )
```

```python
import functools
import math

import jax
import jax.numpy as jnp
from jax import lax
from jax.experimental import pallas as pl
from jax.experimental.pallas import tpu as pltpu
from jax.sharding import PartitionSpec as P

MESH = pl.DeviceIdType.MESH
STEPS = 4
DEL = 4
SM = 3
AHEAD = 2
WIRE = jnp.bfloat16


def ring_distance(offset, size):
    return min(offset, size - offset)


def kernel(
    sizes,
    pair_hbm,
    tile_hbm,
    history_hbm,
    excitation_hbm,
    diagonal_hbm,
    out_ref,
    pairs,
    tiles,
    turned,
    history,
    excitation,
    diagonal,
    by_z,
    near_col,
    far_col,
    drain,
    lhs,
    table,
    product,
    fresh_out,
    fresh_in,
    forward_out,
    forward_in,
    back_out,
    back_in,
    local_sem,
    swap_recv,
    swap_send,
    density_send,
    sum_send,
    fresh_send,
    fresh_recv,
    early_z,
    early_col,
    early_relay,
    early_turn,
    z_recv,
    col_recv,
    forward_recv,
    back_recv,
):
    depth, rows_y, rows_x, slots, clusters, half = sizes
    cols = rows_y * rows_x
    width = 128
    count = 2 * clusters
    stack = 2 * slots
    pair = lax.axis_index("pairs")
    col = lax.axis_index("cols")
    z, core = pair // 2, lax.rem(pair, 2)
    y, x = col // rows_x, lax.rem(col, rows_x)
    sibling = (z * 2 + 1 - core, col)

    def at_z(dz):
        return lax.rem(z + dz, depth)

    def z_device(dz):
        return (at_z(dz) * 2 + core, col)

    def at_col(dy, dx):
        return lax.rem(y + dy, rows_y) * rows_x + lax.rem(x + dx, rows_x)

    def z_distance(dz):
        return ring_distance(dz, depth)

    def col_distance(d):
        return ring_distance(d[0], rows_y) + ring_distance(d[1], rows_x)

    z_near = sorted(range(1, depth), key=z_distance)
    z_far = z_near[::-1]
    col_near = sorted(
        [(dy, dx) for dy in range(rows_y) for dx in range(rows_x)][1:], key=col_distance
    )
    col_far = col_near[::-1]
    z_close = sum(z_distance(d) <= 2 for d in z_near)
    col_close = sum(col_distance(d) <= 2 for d in col_near)
    peers = [z_device(dz) for dz in z_far] + [sibling]
    peers += [(pair, at_col(dy, dx)) for dy, dx in col_far]

    barrier = pltpu.get_barrier_semaphore()
    for peer in peers:
        pl.semaphore_signal(barrier, inc=1, device_id=peer, device_id_type=MESH)

    mine = pl.ds(core * clusters, clusters)
    kept = pl.ds(pl.multiple_of(core * half, half), half)
    given = pl.ds(pl.multiple_of((1 - core) * half, half), half)

    def column(s):
        return pl.ds(pl.multiple_of((core * slots + s) * width, width), width)

    loads = [
        pltpu.make_async_copy(
            history_hbm.at[:, :, kept, :], history.at[:, mine], local_sem.at[0]
        ),
        pltpu.make_async_copy(pair_hbm, pairs.at[core], local_sem.at[1]),
        pltpu.make_async_copy(
            excitation_hbm.at[:, :, kept, :], excitation.at[:, mine], local_sem.at[2]
        ),
        pltpu.make_async_copy(diagonal_hbm, diagonal.at[core], local_sem.at[3]),
    ]
    for load in loads:
        load.start()
    for s in range(slots):
        pltpu.make_async_copy(
            tile_hbm.at[s], tiles.at[:, column(s)], local_sem.at[4]
        ).start()

    def round_history(who):
        part = pl.ds(who * clusters, clusters)
        for d in range(DEL):
            rounded = history[d, part].astype(jnp.bfloat16)
            by_z[DEL - 1 - d, z, part] = rounded
            near_col[DEL - 1 - d, 0, part] = rounded

    loads[0].wait()
    round_history(core)

    pl.semaphore_wait(barrier, len(peers))

    def copy(src, dst, send, recv, device):
        return pltpu.make_async_remote_copy(
            src_ref=src,
            dst_ref=dst,
            send_sem=send,
            recv_sem=recv,
            device_id=device,
            device_id_type=MESH,
        )

    swaps = [
        copy(
            history_hbm.at[:, :, given, :],
            history.at[:, mine],
            swap_send.at[0],
            swap_recv.at[0],
            sibling,
        ),
        copy(pair_hbm, pairs.at[core], swap_send.at[1], swap_recv.at[1], sibling),
        copy(
            excitation_hbm.at[:, :, given, :],
            excitation.at[:, mine],
            swap_send.at[2],
            swap_recv.at[2],
            sibling,
        ),
        copy(diagonal_hbm, diagonal.at[core], swap_send.at[3], swap_recv.at[3], sibling),
    ]
    for swap in swaps:
        swap.start()

    def arrival(times, index, part):
        if index < col_close:
            return near_col.at[times, index + 1, part]
        return far_col.at[times, index - col_close, part]

    def send_density(times, part, z_sem, col_sem):
        source = by_z.at[times, z, part]
        for dz in z_far:
            copy(source, source, density_send, z_sem, z_device(dz)).start()
        for offset in col_far:
            index = col_near.index(offset)
            group = 0 if index < col_close else 1
            target = (pair, at_col(*offset))
            sem = col_sem(group)
            copy(source, arrival(times, index, part), density_send, sem, target).start()

    def wait_recv(ref, sem):
        copy(ref, ref, density_send, sem, sibling).wait_recv()

    past = pl.ds(0, DEL)
    relay_z = [dz for dz in z_near if z_distance(dz) == 2] if depth == 8 else []
    direct_z = [dz for dz in z_far if z_distance(dz) <= 2 or not relay_z]
    x_line = [(0, dx) for dx in range(1, rows_x)]
    y_line = [(dy, 0) for dy in range(1, rows_y)]
    lines = [offset for offset in col_far if 0 in offset]

    def early_first(way, part):
        source = by_z.at[past, z, part]
        for dz in direct_z:
            sem = early_z
            if dz in relay_z:
                sem = early_relay.at[way, relay_z.index(dz)]
            copy(source, source, density_send, sem, z_device(dz)).start()
        first = x_line if way == 0 else y_line
        for offset in lines:
            sem = early_col
            if offset in first:
                sem = early_turn.at[way, first.index(offset)]
            target = arrival(past, col_near.index(offset), part)
            copy(source, target, density_send, sem, (pair, at_col(*offset))).start()

    def early_relays(way, part):
        first, second = (x_line, y_line) if way == 0 else (y_line, x_line)
        for start in sorted(first, key=col_distance):
            block = arrival(past, col_near.index(start), part)
            wait_recv(block, early_turn.at[way, first.index(start)])
            for then in sorted(second, key=lambda d: -col_distance(d)):
                final = (start[0] + then[0], start[1] + then[1])
                target = arrival(past, col_near.index(final), part)
                copy(block, target, density_send, early_col, (pair, at_col(*then))).start()
        for index, dz in enumerate(relay_z):
            block = by_z.at[past, at_z(depth - dz), part]
            wait_recv(block, early_relay.at[way, index])
            unit = dz // 2 if dz == 2 else depth - 1
            if (dz == 2) == (way == 0):
                copy(block, block, density_send, early_z, z_device(dz)).start()
            copy(block, block, density_send, early_z, z_device(unit)).start()

    theirs = pl.ds((1 - core) * clusters, clusters)
    early_first(0, mine)
    for s in range(slots):
        copy(
            tile_hbm.at[s], tiles.at[:, column(s)], swap_send.at[4], swap_recv.at[4], sibling
        ).start()
    swaps[0].wait_recv()
    round_history(1 - core)
    early_first(1, theirs)

    for load in loads[1:]:
        load.wait()
    for swap in swaps[1:]:
        swap.wait_recv()

    def field_of(s, k):
        return pairs[s // slots, s % slots, k]

    keys = [
        jnp.where(field_of(s, 4) == 1, field_of(s, 1) * clusters + field_of(s, 2), -1)
        for s in range(stack)
    ]

    def place(n, carry):
        dz, rest = n // count, lax.rem(n, count)
        key = at_z(dz) * count + rest
        seen = jnp.int32(0)
        found = [jnp.int32(stack)] * (2 * SM)
        for s in range(stack):
            hit = keys[s] == key
            found = [jnp.where(hit & (seen == k), s, found[k]) for k in range(2 * SM)]
            seen = jnp.where(hit, seen + 1, seen)
        for k in range(2 * SM):
            table[n * 2 * SM + k] = found[k]
        return carry

    lax.fori_loop(0, depth * count, place, 0)
    product[stack] = jnp.zeros_like(product[stack])

    def turn(who):
        part = pl.ds(pl.multiple_of(who * slots * width, width), slots * width)

        def body(c, carry):
            rows = pl.ds(pl.multiple_of(c * width, width), width)
            turned[c, part, :] = tiles[rows, part].T
            return carry

        lax.fori_loop(0, cols, body, 0)

    held = tiles.at[:, pl.ds(0, slots * width)]
    pltpu.make_async_copy(held, held, local_sem.at[4]).wait()
    early_relays(0, mine)
    early_relays(1, theirs)
    turn(core)
    wait_recv(held, swap_recv.at[4])
    turn(1 - core)

    others = DEL * (2 * (cols - 1) - len(x_line) - len(y_line)) // 2
    wait_recv(drain.at[pl.ds(0, others)], early_col)
    wait_recv(drain.at[pl.ds(0, DEL * (depth - 1 - len(relay_z)))], early_z)

    def tile_rows(offset):
        source = at_col(rows_y - offset[0], rows_x - offset[1])
        return pl.ds(pl.multiple_of(source * width, width), width)

    def backward(s, t, blocks, offsets):
        when = t + DEL - 1 - field_of(s, 3)
        which = s // slots * clusters + field_of(s, 0)
        total = None
        for first in range(0, len(offsets), 2):
            span = range(first, min(first + 2, len(offsets)))
            near = [blocks[when, k, which] for k in span]
            tile = [tiles[tile_rows(offsets[k]), s * width : (s + 1) * width] for k in span]
            part = jnp.dot(
                jnp.concatenate(near, axis=1),
                jnp.concatenate(tile, axis=0),
                preferred_element_type=jnp.float32,
            )
            total = part if total is None else total + part
        return total

    def combine(dz, j):
        base = (dz * count + j) * 2 * SM
        total = product[table[base]]
        for k in range(1, 2 * SM):
            total += product[table[base + k]]
        return total

    def step(t, carry):
        times = pl.ds(DEL - 1 + t, 1)

        @pl.when(t > 0)
        def near_arrived():
            wait_recv(near_col.at[times, pl.ds(1, col_close)], col_recv.at[t, 0])

        near_offsets = [(0, 0)] + col_near[:col_close]
        for s in range(stack):
            product[s] = backward(s, t, near_col, near_offsets)

        @pl.when(t > 0)
        def z_arrived():
            wait_recv(by_z.at[times, pl.ds(0, depth - 1)], z_recv.at[t])

        for s in range(stack):
            when = t + DEL - 1 - field_of(s, 3)
            owner = field_of(s, 1)
            which = lax.rem(owner, 2) * clusters + field_of(s, 2)
            block = by_z[when, owner // 2, which]
            for l in range(clusters):
                chosen = (field_of(s, 4) == 1) & (field_of(s, 0) == l)
                for who in range(2):
                    row = (who * clusters + l) * half
                    value = jnp.zeros_like(block)
                    if who == s // slots:
                        value = jnp.where(chosen, block, value)
                    lhs[row : row + half, s * width : (s + 1) * width] = value

        far_offsets = col_near[col_close:]
        if far_offsets:

            @pl.when(t > 0)
            def far_arrived():
                wait_recv(far_col.at[times], col_recv.at[t, 1])

            for s in range(stack):
                product[s] += backward(s, t, far_col, far_offsets)

        for dz in z_far:
            index = z_near.index(dz)
            for j in range(count):
                back_out[t, index, j] = combine(dz, j).astype(WIRE)
            copy(
                back_out.at[t, index],
                back_in.at[t, index],
                sum_send,
                back_recv.at[t, 0 if index < z_close else 1],
                z_device(dz),
            ).start()

        left = lhs[...]

        def forward(offset):
            return jnp.dot(
                left, turned[at_col(*offset)], preferred_element_type=jnp.float32
            ).reshape(count, half, width)

        def send_forward(offset, part):
            index = col_near.index(offset)
            forward_out[t, index] = part.astype(WIRE)
            copy(
                forward_out.at[t, index],
                forward_in.at[t, index],
                sum_send,
                forward_recv.at[t, 0 if index < col_close else 1],
                (pair, at_col(*offset)),
            ).start()

        waiting = []
        for offset in col_far:
            waiting.append((offset, forward(offset)))
            if len(waiting) > AHEAD:
                send_forward(*waiting.pop(0))
        field = forward((0, 0))
        for item in waiting:
            send_forward(*item)
        field = field + jnp.stack([combine(0, j) for j in range(count)])

        def collect(field, ref, first, last, sem):
            if last > first:
                wait_recv(ref.at[t, pl.ds(first, last - first)], sem)
                for index in range(first, last):
                    field = field + ref[t, index].astype(jnp.float32)
            return field

        field = collect(field, back_in, 0, z_close, back_recv.at[t, 0])
        field = collect(field, back_in, z_close, depth - 1, back_recv.at[t, 1])
        field = collect(field, forward_in, 0, col_close, forward_recv.at[t, 0])
        field = collect(field, forward_in, col_close, cols - 1, forward_recv.at[t, 1])
        weights = diagonal[...].reshape(count, 1, width)
        fresh = (excitation[t] - field) / weights
        fresh_out[t] = fresh

        @pl.when(t < STEPS - 1)
        def publish():
            rounded = fresh.astype(jnp.bfloat16)
            by_z[DEL + t, z] = rounded
            near_col[DEL + t, 0] = rounded
            send_density(
                pl.ds(DEL + t, 1),
                pl.ds(0, count),
                z_recv.at[t + 1],
                lambda group: col_recv.at[t + 1, group],
            )

        copy(
            fresh_out.at[t, pl.ds((1 - core) * clusters, clusters)],
            fresh_in.at[t],
            fresh_send,
            fresh_recv,
            sibling,
        ).start()
        out_ref[t, :, kept, :] = fresh_out[t, mine]
        return carry

    lax.fori_loop(0, STEPS, step, 0)

    def sent(ref, sem):
        copy(ref, ref, sem, fresh_recv, sibling).wait_send()

    for swap in swaps:
        swap.wait_send()
    sent(held, swap_send.at[4])
    sent(drain.at[pl.ds(0, (DEL + STEPS - 1) * (depth - 1 + cols - 1))], density_send)
    sent(drain.at[pl.ds(0, STEPS * (depth - 1 + cols - 1))], sum_send)
    sent(fresh_in, fresh_send)
    wait_recv(fresh_in, fresh_recv)
    for t in range(STEPS):
        out_ref[t, :, given, :] = fresh_in[t]


def march(groups, cols, pair_list, near_tile_block, history, excitation, diagonal):
    slots, patches, width = near_tile_block.shape
    clusters, excite = history.shape[1:3]
    depth = groups // 2
    half = excite // 2
    rows_y = rows_x = math.isqrt(cols)
    near = 1 + sum(
        0 < ring_distance(dy, rows_y) + ring_distance(dx, rows_x) <= 2
        for dy in range(rows_y)
        for dx in range(rows_x)
    )
    block = (2 * clusters, half, width)
    dma = pltpu.SemaphoreType.DMA
    times = DEL + STEPS - 1
    anywhere = pl.BlockSpec(memory_space=pl.ANY)
    return pl.pallas_call(
        functools.partial(kernel, (depth, rows_y, rows_x, slots, clusters, half)),
        out_shape=OUT((STEPS, clusters, excite, width), jnp.float32),
        in_specs=[anywhere] * 5,
        out_specs=pl.BlockSpec(memory_space=pltpu.VMEM),
        scratch_shapes=[
            pltpu.SMEM((2,) + pair_list.shape, jnp.int32),
            pltpu.VMEM((patches, 2 * slots * width), jnp.bfloat16),
            pltpu.VMEM((cols, 2 * slots * width, width), jnp.bfloat16),
            pltpu.VMEM((DEL,) + block, jnp.float32),
            pltpu.VMEM((STEPS,) + block, jnp.float32),
            pltpu.VMEM((2, clusters, width), jnp.float32),
            pltpu.VMEM((times, depth) + block, jnp.bfloat16),
            pltpu.VMEM((times, near) + block, jnp.bfloat16),
            pltpu.VMEM((times, max(cols - near, 1)) + block, jnp.bfloat16),
            pltpu.VMEM((times * (depth + cols),) + block, WIRE),
            pltpu.VMEM((2 * clusters * half, 2 * slots * width), jnp.bfloat16),
            pltpu.SMEM((depth * 2 * clusters * 2 * SM,), jnp.int32),
            pltpu.VMEM((2 * slots + 1, half, width), jnp.float32),
            pltpu.VMEM((STEPS,) + block, jnp.float32),
            pltpu.VMEM((STEPS, clusters, half, width), jnp.float32),
            pltpu.VMEM((STEPS, cols - 1) + block, WIRE),
            pltpu.VMEM((STEPS, cols - 1) + block, WIRE),
            pltpu.VMEM((STEPS, depth - 1) + block, WIRE),
            pltpu.VMEM((STEPS, depth - 1) + block, WIRE),
            dma((5,)),
            dma((5,)),
            dma((5,)),
            dma,
            dma,
            dma,
            dma,
            dma,
            dma,
            dma((2, 2)),
            dma((2, rows_x - 1)),
            dma((STEPS,)),
            dma((STEPS, 2)),
            dma((STEPS, 2)),
            dma((STEPS, 2)),
        ],
        compiler_params=pltpu.CompilerParams(collective_id=0, has_side_effects=True),
    )(pair_list, near_tile_block, history, excitation, diagonal)


OUT = pltpu.VMEM


def solution(mesh):
    placed = (
        P("pairs", None),
        P("pairs", None, "cols"),
        P(None, "pairs", None, "cols"),
        P(None, "pairs", None, "cols"),
        P("pairs", "cols"),
    )
    return jax.shard_map(
        functools.partial(march, mesh.shape["pairs"], mesh.shape["cols"]),
        mesh=mesh,
        in_specs=placed,
        out_specs=P(None, "pairs", None, "cols"),
        check_vma=False,
    )
```

```python
import functools
import math

import jax
import jax.numpy as jnp
from jax import lax
from jax.experimental import pallas as pl
from jax.experimental.pallas import tpu as pltpu
from jax.sharding import PartitionSpec as P

MESH = pl.DeviceIdType.MESH
STEPS = 4
DEL = 4
SM = 3
AHEAD = 2
WIRE = jnp.bfloat16


def ring_distance(offset, size):
    return min(offset, size - offset)


def kernel(
    sizes,
    pair_hbm,
    tile_hbm,
    history_hbm,
    excitation_hbm,
    diagonal_hbm,
    out_ref,
    pairs,
    tiles,
    turned,
    history,
    excitation,
    diagonal,
    by_z,
    near_col,
    far_col,
    drain,
    lhs,
    table,
    product,
    fresh_out,
    fresh_in,
    forward_out,
    forward_in,
    back_out,
    back_in,
    local_sem,
    swap_recv,
    swap_send,
    density_send,
    sum_send,
    fresh_send,
    fresh_recv,
    early_z,
    early_col,
    early_relay,
    early_turn,
    z_recv,
    col_recv,
    forward_recv,
    back_recv,
):
    depth, rows_y, rows_x, slots, clusters, half = sizes
    cols = rows_y * rows_x
    width = 128
    count = 2 * clusters
    stack = 2 * slots
    pair = lax.axis_index("pairs")
    col = lax.axis_index("cols")
    z, core = pair // 2, lax.rem(pair, 2)
    y, x = col // rows_x, lax.rem(col, rows_x)
    sibling = (z * 2 + 1 - core, col)

    def at_z(dz):
        return lax.rem(z + dz, depth)

    def z_device(dz):
        return (at_z(dz) * 2 + core, col)

    def at_col(dy, dx):
        return lax.rem(y + dy, rows_y) * rows_x + lax.rem(x + dx, rows_x)

    def z_distance(dz):
        return ring_distance(dz, depth)

    def col_distance(d):
        return ring_distance(d[0], rows_y) + ring_distance(d[1], rows_x)

    z_near = sorted(range(1, depth), key=z_distance)
    z_far = z_near[::-1]
    col_near = sorted(
        [(dy, dx) for dy in range(rows_y) for dx in range(rows_x)][1:], key=col_distance
    )
    col_far = col_near[::-1]
    z_close = sum(z_distance(d) <= 2 for d in z_near)
    col_close = sum(col_distance(d) <= 2 for d in col_near)
    peers = [z_device(dz) for dz in z_far] + [sibling]
    peers += [(pair, at_col(dy, dx)) for dy, dx in col_far]

    barrier = pltpu.get_barrier_semaphore()
    for peer in peers:
        pl.semaphore_signal(barrier, inc=1, device_id=peer, device_id_type=MESH)

    mine = pl.ds(core * clusters, clusters)
    kept = pl.ds(pl.multiple_of(core * half, half), half)
    given = pl.ds(pl.multiple_of((1 - core) * half, half), half)

    def column(s):
        return pl.ds(pl.multiple_of((core * slots + s) * width, width), width)

    loads = [
        pltpu.make_async_copy(
            history_hbm.at[:, :, kept, :], history.at[:, mine], local_sem.at[0]
        ),
        pltpu.make_async_copy(pair_hbm, pairs.at[core], local_sem.at[1]),
        pltpu.make_async_copy(
            excitation_hbm.at[:, :, kept, :], excitation.at[:, mine], local_sem.at[2]
        ),
        pltpu.make_async_copy(diagonal_hbm, diagonal.at[core], local_sem.at[3]),
    ]
    for load in loads:
        load.start()
    for s in range(slots):
        pltpu.make_async_copy(
            tile_hbm.at[s], tiles.at[:, column(s)], local_sem.at[4]
        ).start()

    def round_history(who):
        part = pl.ds(who * clusters, clusters)
        for d in range(DEL):
            rounded = history[d, part].astype(jnp.bfloat16)
            by_z[DEL - 1 - d, z, part] = rounded
            near_col[DEL - 1 - d, 0, part] = rounded

    loads[0].wait()
    round_history(core)

    pl.semaphore_wait(barrier, len(peers))

    def copy(src, dst, send, recv, device):
        return pltpu.make_async_remote_copy(
            src_ref=src,
            dst_ref=dst,
            send_sem=send,
            recv_sem=recv,
            device_id=device,
            device_id_type=MESH,
        )

    swaps = [
        copy(
            history_hbm.at[:, :, given, :],
            history.at[:, mine],
            swap_send.at[0],
            swap_recv.at[0],
            sibling,
        ),
        copy(pair_hbm, pairs.at[core], swap_send.at[1], swap_recv.at[1], sibling),
        copy(
            excitation_hbm.at[:, :, given, :],
            excitation.at[:, mine],
            swap_send.at[2],
            swap_recv.at[2],
            sibling,
        ),
        copy(diagonal_hbm, diagonal.at[core], swap_send.at[3], swap_recv.at[3], sibling),
    ]
    for swap in swaps:
        swap.start()

    def arrival(times, index, part):
        if index < col_close:
            return near_col.at[times, index + 1, part]
        return far_col.at[times, index - col_close, part]

    def send_density(times, part, z_sem, col_sem):
        source = by_z.at[times, z, part]
        for offset in col_far[:5]:
            index = col_near.index(offset)
            group = 0 if index < col_close else 1
            target = (pair, at_col(*offset))
            sem = col_sem(group)
            copy(source, arrival(times, index, part), density_send, sem, target).start()
        for dz in z_far:
            copy(source, source, density_send, z_sem, z_device(dz)).start()
        for offset in col_far[5:]:
            index = col_near.index(offset)
            group = 0 if index < col_close else 1
            target = (pair, at_col(*offset))
            sem = col_sem(group)
            copy(source, arrival(times, index, part), density_send, sem, target).start()

    def wait_recv(ref, sem):
        copy(ref, ref, density_send, sem, sibling).wait_recv()

    past = pl.ds(0, DEL)
    relay_z = [dz for dz in z_near if z_distance(dz) == 2] if depth == 8 else []
    direct_z = [dz for dz in z_far if z_distance(dz) <= 2 or not relay_z]
    x_line = [(0, dx) for dx in range(1, rows_x)]
    y_line = [(dy, 0) for dy in range(1, rows_y)]
    lines = [offset for offset in col_far if 0 in offset]

    def early_first(way, part):
        source = by_z.at[past, z, part]
        for dz in direct_z:
            sem = early_z
            if dz in relay_z:
                sem = early_relay.at[way, relay_z.index(dz)]
            copy(source, source, density_send, sem, z_device(dz)).start()
        first = x_line if way == 0 else y_line
        for offset in lines:
            sem = early_col
            if offset in first:
                sem = early_turn.at[way, first.index(offset)]
            target = arrival(past, col_near.index(offset), part)
            copy(source, target, density_send, sem, (pair, at_col(*offset))).start()

    def early_relays(way, part):
        first, second = (x_line, y_line) if way == 0 else (y_line, x_line)
        for start in sorted(first, key=col_distance):
            block = arrival(past, col_near.index(start), part)
            wait_recv(block, early_turn.at[way, first.index(start)])
            for then in sorted(second, key=lambda d: -col_distance(d)):
                final = (start[0] + then[0], start[1] + then[1])
                target = arrival(past, col_near.index(final), part)
                copy(block, target, density_send, early_col, (pair, at_col(*then))).start()
        for index, dz in enumerate(relay_z):
            block = by_z.at[past, at_z(depth - dz), part]
            wait_recv(block, early_relay.at[way, index])
            unit = dz // 2 if dz == 2 else depth - 1
            if (dz == 2) == (way == 0):
                copy(block, block, density_send, early_z, z_device(dz)).start()
            copy(block, block, density_send, early_z, z_device(unit)).start()

    theirs = pl.ds((1 - core) * clusters, clusters)
    early_first(0, mine)
    for s in range(slots):
        copy(
            tile_hbm.at[s], tiles.at[:, column(s)], swap_send.at[4], swap_recv.at[4], sibling
        ).start()
    swaps[0].wait_recv()
    round_history(1 - core)
    early_first(1, theirs)

    for load in loads[1:]:
        load.wait()
    for swap in swaps[1:]:
        swap.wait_recv()

    def field_of(s, k):
        return pairs[s // slots, s % slots, k]

    keys = [
        jnp.where(field_of(s, 4) == 1, field_of(s, 1) * clusters + field_of(s, 2), -1)
        for s in range(stack)
    ]

    def place(n, carry):
        dz, rest = n // count, lax.rem(n, count)
        key = at_z(dz) * count + rest
        seen = jnp.int32(0)
        found = [jnp.int32(stack)] * (2 * SM)
        for s in range(stack):
            hit = keys[s] == key
            found = [jnp.where(hit & (seen == k), s, found[k]) for k in range(2 * SM)]
            seen = jnp.where(hit, seen + 1, seen)
        for k in range(2 * SM):
            table[n * 2 * SM + k] = found[k]
        return carry

    lax.fori_loop(0, depth * count, place, 0)
    product[stack] = jnp.zeros_like(product[stack])

    def turn(who):
        part = pl.ds(pl.multiple_of(who * slots * width, width), slots * width)

        def body(c, carry):
            rows = pl.ds(pl.multiple_of(c * width, width), width)
            turned[c, part, :] = tiles[rows, part].T
            return carry

        lax.fori_loop(0, cols, body, 0)

    held = tiles.at[:, pl.ds(0, slots * width)]
    pltpu.make_async_copy(held, held, local_sem.at[4]).wait()
    early_relays(0, mine)
    early_relays(1, theirs)
    turn(core)
    wait_recv(held, swap_recv.at[4])
    turn(1 - core)

    others = DEL * (2 * (cols - 1) - len(x_line) - len(y_line)) // 2
    wait_recv(drain.at[pl.ds(0, others)], early_col)
    wait_recv(drain.at[pl.ds(0, DEL * (depth - 1 - len(relay_z)))], early_z)

    def tile_rows(offset):
        source = at_col(rows_y - offset[0], rows_x - offset[1])
        return pl.ds(pl.multiple_of(source * width, width), width)

    def backward(s, t, blocks, offsets):
        when = t + DEL - 1 - field_of(s, 3)
        which = s // slots * clusters + field_of(s, 0)
        total = None
        for first in range(0, len(offsets), 2):
            span = range(first, min(first + 2, len(offsets)))
            near = [blocks[when, k, which] for k in span]
            tile = [tiles[tile_rows(offsets[k]), s * width : (s + 1) * width] for k in span]
            part = jnp.dot(
                jnp.concatenate(near, axis=1),
                jnp.concatenate(tile, axis=0),
                preferred_element_type=jnp.float32,
            )
            total = part if total is None else total + part
        return total

    def combine(dz, j):
        base = (dz * count + j) * 2 * SM
        total = product[table[base]]
        for k in range(1, 2 * SM):
            total += product[table[base + k]]
        return total

    def step(t, carry):
        times = pl.ds(DEL - 1 + t, 1)

        @pl.when(t > 0)
        def near_arrived():
            wait_recv(near_col.at[times, pl.ds(1, col_close)], col_recv.at[t, 0])

        near_offsets = [(0, 0)] + col_near[:col_close]
        for s in range(stack):
            product[s] = backward(s, t, near_col, near_offsets)

        @pl.when(t > 0)
        def z_arrived():
            wait_recv(by_z.at[times, pl.ds(0, depth - 1)], z_recv.at[t])

        for s in range(stack):
            when = t + DEL - 1 - field_of(s, 3)
            owner = field_of(s, 1)
            which = lax.rem(owner, 2) * clusters + field_of(s, 2)
            block = by_z[when, owner // 2, which]
            for l in range(clusters):
                chosen = (field_of(s, 4) == 1) & (field_of(s, 0) == l)
                for who in range(2):
                    row = (who * clusters + l) * half
                    value = jnp.zeros_like(block)
                    if who == s // slots:
                        value = jnp.where(chosen, block, value)
                    lhs[row : row + half, s * width : (s + 1) * width] = value

        far_offsets = col_near[col_close:]
        if far_offsets:

            @pl.when(t > 0)
            def far_arrived():
                wait_recv(far_col.at[times], col_recv.at[t, 1])

            for s in range(stack):
                product[s] += backward(s, t, far_col, far_offsets)

        for dz in z_far:
            index = z_near.index(dz)
            for j in range(count):
                back_out[t, index, j] = combine(dz, j).astype(WIRE)
            copy(
                back_out.at[t, index],
                back_in.at[t, index],
                sum_send,
                back_recv.at[t, 0 if index < z_close else 1],
                z_device(dz),
            ).start()

        left = lhs[...]

        def forward(offset):
            return jnp.dot(
                left, turned[at_col(*offset)], preferred_element_type=jnp.float32
            ).reshape(count, half, width)

        def send_forward(offset, part):
            index = col_near.index(offset)
            forward_out[t, index] = part.astype(WIRE)
            copy(
                forward_out.at[t, index],
                forward_in.at[t, index],
                sum_send,
                forward_recv.at[t, 0 if index < col_close else 1],
                (pair, at_col(*offset)),
            ).start()

        waiting = []
        for offset in col_far:
            waiting.append((offset, forward(offset)))
            if len(waiting) > AHEAD:
                send_forward(*waiting.pop(0))
        field = forward((0, 0))
        for item in waiting:
            send_forward(*item)
        field = field + jnp.stack([combine(0, j) for j in range(count)])

        def collect(field, ref, first, last, sem):
            if last > first:
                wait_recv(ref.at[t, pl.ds(first, last - first)], sem)
                for index in range(first, last):
                    field = field + ref[t, index].astype(jnp.float32)
            return field

        field = collect(field, back_in, 0, z_close, back_recv.at[t, 0])
        field = collect(field, back_in, z_close, depth - 1, back_recv.at[t, 1])
        field = collect(field, forward_in, 0, col_close, forward_recv.at[t, 0])
        field = collect(field, forward_in, col_close, cols - 1, forward_recv.at[t, 1])
        weights = diagonal[...].reshape(count, 1, width)
        fresh = (excitation[t] - field) / weights
        fresh_out[t] = fresh

        @pl.when(t < STEPS - 1)
        def publish():
            rounded = fresh.astype(jnp.bfloat16)
            by_z[DEL + t, z] = rounded
            near_col[DEL + t, 0] = rounded
            send_density(
                pl.ds(DEL + t, 1),
                pl.ds(0, count),
                z_recv.at[t + 1],
                lambda group: col_recv.at[t + 1, group],
            )

        copy(
            fresh_out.at[t, pl.ds((1 - core) * clusters, clusters)],
            fresh_in.at[t],
            fresh_send,
            fresh_recv,
            sibling,
        ).start()
        out_ref[t, :, kept, :] = fresh_out[t, mine]
        return carry

    lax.fori_loop(0, STEPS, step, 0)

    def sent(ref, sem):
        copy(ref, ref, sem, fresh_recv, sibling).wait_send()

    for swap in swaps:
        swap.wait_send()
    sent(held, swap_send.at[4])
    sent(drain.at[pl.ds(0, (DEL + STEPS - 1) * (depth - 1 + cols - 1))], density_send)
    sent(drain.at[pl.ds(0, STEPS * (depth - 1 + cols - 1))], sum_send)
    sent(fresh_in, fresh_send)
    wait_recv(fresh_in, fresh_recv)
    for t in range(STEPS):
        out_ref[t, :, given, :] = fresh_in[t]


def march(groups, cols, pair_list, near_tile_block, history, excitation, diagonal):
    slots, patches, width = near_tile_block.shape
    clusters, excite = history.shape[1:3]
    depth = groups // 2
    half = excite // 2
    rows_y = rows_x = math.isqrt(cols)
    near = 1 + sum(
        0 < ring_distance(dy, rows_y) + ring_distance(dx, rows_x) <= 2
        for dy in range(rows_y)
        for dx in range(rows_x)
    )
    block = (2 * clusters, half, width)
    dma = pltpu.SemaphoreType.DMA
    times = DEL + STEPS - 1
    anywhere = pl.BlockSpec(memory_space=pl.ANY)
    return pl.pallas_call(
        functools.partial(kernel, (depth, rows_y, rows_x, slots, clusters, half)),
        out_shape=OUT((STEPS, clusters, excite, width), jnp.float32),
        in_specs=[anywhere] * 5,
        out_specs=pl.BlockSpec(memory_space=pltpu.VMEM),
        scratch_shapes=[
            pltpu.SMEM((2,) + pair_list.shape, jnp.int32),
            pltpu.VMEM((patches, 2 * slots * width), jnp.bfloat16),
            pltpu.VMEM((cols, 2 * slots * width, width), jnp.bfloat16),
            pltpu.VMEM((DEL,) + block, jnp.float32),
            pltpu.VMEM((STEPS,) + block, jnp.float32),
            pltpu.VMEM((2, clusters, width), jnp.float32),
            pltpu.VMEM((times, depth) + block, jnp.bfloat16),
            pltpu.VMEM((times, near) + block, jnp.bfloat16),
            pltpu.VMEM((times, max(cols - near, 1)) + block, jnp.bfloat16),
            pltpu.VMEM((times * (depth + cols),) + block, WIRE),
            pltpu.VMEM((2 * clusters * half, 2 * slots * width), jnp.bfloat16),
            pltpu.SMEM((depth * 2 * clusters * 2 * SM,), jnp.int32),
            pltpu.VMEM((2 * slots + 1, half, width), jnp.float32),
            pltpu.VMEM((STEPS,) + block, jnp.float32),
            pltpu.VMEM((STEPS, clusters, half, width), jnp.float32),
            pltpu.VMEM((STEPS, cols - 1) + block, WIRE),
            pltpu.VMEM((STEPS, cols - 1) + block, WIRE),
            pltpu.VMEM((STEPS, depth - 1) + block, WIRE),
            pltpu.VMEM((STEPS, depth - 1) + block, WIRE),
            dma((5,)),
            dma((5,)),
            dma((5,)),
            dma,
            dma,
            dma,
            dma,
            dma,
            dma,
            dma((2, 2)),
            dma((2, rows_x - 1)),
            dma((STEPS,)),
            dma((STEPS, 2)),
            dma((STEPS, 2)),
            dma((STEPS, 2)),
        ],
        compiler_params=pltpu.CompilerParams(collective_id=0, has_side_effects=True),
    )(pair_list, near_tile_block, history, excitation, diagonal)


OUT = pltpu.VMEM


def solution(mesh):
    placed = (
        P("pairs", None),
        P("pairs", None, "cols"),
        P(None, "pairs", None, "cols"),
        P(None, "pairs", None, "cols"),
        P("pairs", "cols"),
    )
    return jax.shard_map(
        functools.partial(march, mesh.shape["pairs"], mesh.shape["cols"]),
        mesh=mesh,
        in_specs=placed,
        out_specs=P(None, "pairs", None, "cols"),
        check_vma=False,
    )
```
